32 devices in a mesh: pipe: 4 (over y, x), row: 2 (over core), col: 4 (over z).
Axes of the slice: x: 2, y: 2, z: 4, core: 2. Of those that a mesh axis runs over, the one named last changes fastest.
Arguments:
- act_handoff: bfloat16 [4, 512, 4096], P('pipe', 'col', 'row'), may hold values from -6 to 6
- grad_handoff: bfloat16 [4, 512, 4096], P('pipe', 'col', 'row'), may hold values from -6 to 6
- up_blocks: bfloat16 [4, 2, 4, 1024, 4096], P('pipe', 'row', 'col'), may hold values from -0.125 to 0.125
- down_blocks: bfloat16 [4, 2, 4, 1024, 4096], P('pipe', 'row', 'col'), may hold values from -0.0625 to 0.0625
- up_mask: int32 [4, 64, 224], P('pipe', 'row', 'col'), may hold values from 0 to 1, as said below
- down_mask: int32 [4, 224, 64], P('pipe', 'col', 'row'), may hold values from 0 to 1, as said below
Outputs:
- section_output: bfloat16 [4, 512, 4096], P('pipe', 'col', 'row')
- input_grad: bfloat16 [4, 512, 4096], P('pipe', 'col', 'row')
- up_grad: bfloat16 [4, 2, 4, 1024, 4096], P('pipe', 'row', 'col')
- down_grad: bfloat16 [4, 2, 4, 1024, 4096], P('pipe', 'row', 'col')
The draws below stay inside these ranges and needn't reach their ends.
Inputs may be any that keep to these rules, and one draw needn't show every extreme that they name: `up_mask`: per section, every tile of either mask holds at most 1024 live blocks and at least 560, and in every section some tile holds exactly 1024. `down_mask`: as for up_mask, with tiles of 56 x 32 blocks.
All inputs are finite; a program needn't handle non-finite values.
Results may differ from the reference program's by a relative error of at most 0.013.
Values may be sent and summed in bfloat16 or wider, within the bound.
No kernel may reach another device: no remote copies, remote signals or barrier semaphores. Data moves between devices by JAX's collectives and lax.ppermute only.
A program may use at most 256 MiB of HBM per device.

```python
import jax
import jax.numpy as jnp
from jax import lax

D = 4096
FF = 14336
BLK = 64
TOK = 512
BD = 64
BF = 224
TBR = 32
TBC = 56
TILE = 1792
CAP = 1024
N_PIPE = 4
N_ROW = 2
N_COL = 4


def tile_live(key, tile_rows, tile_cols):
    tiles = tile_rows * tile_cols
    groups = N_ROW * N_COL
    key_count, key_pick, key_score = jax.random.split(key, 3)
    counts = jax.random.randint(key_count, (N_PIPE, groups), TILE * 5 // 16, CAP + 1, dtype=jnp.int32)
    chosen = jax.random.randint(key_pick, (N_PIPE,), 0, groups, dtype=jnp.int32)
    places = jnp.arange(groups, dtype=jnp.int32)
    counts = jnp.where(places[None, :] == chosen[:, None], CAP, counts)
    scores = jax.random.randint(key_score, (N_PIPE, groups, tiles), 0, 1 << 18, dtype=jnp.int32)
    scores = scores * 4096 + jnp.arange(tiles, dtype=jnp.int32)[None, None, :]
    ranks = jnp.argsort(jnp.argsort(scores, axis=-1), axis=-1).astype(jnp.int32)
    return (ranks < counts[:, :, None]).astype(jnp.int32)


def draw_up_mask(key, part):
    live = tile_live(jax.random.fold_in(key, 11), TBR, TBC)
    return live.reshape(N_PIPE, N_ROW, N_COL, TBR, TBC).transpose(0, 1, 3, 2, 4).reshape(N_PIPE, BD, BF)


def draw_down_mask(key, part):
    live = tile_live(jax.random.fold_in(key, 23), TBC, TBR)
    return live.reshape(N_PIPE, N_ROW, N_COL, TBC, TBR).transpose(0, 2, 3, 1, 4).reshape(N_PIPE, BF, BD)


def shard_levels(stream_key, dims, cuts, smallest, high):
    level = 1.0
    for dim, parts in cuts:
        heights = jax.random.uniform(jax.random.fold_in(jax.random.fold_in(stream_key, 6), dim), (parts,), jnp.float32, smallest / len(cuts), high / len(cuts))
        level = level * jnp.repeat(jnp.exp(heights), dims[dim] // parts).reshape((-1,) + (1,) * (len(dims) - 1 - dim))
    return level


def scatter_about(key, extent, spread, most, shards=(), kind=jnp.bfloat16):
    entries = jax.random.normal(key, extent, jnp.float32) * spread
    if len(shards) > 0:
        entries = shard_levels(key, extent, shards, -0.22, 0.18) * entries
    return jnp.clip(entries, min=-most, max=most).astype(kind)


def setup_inputs(seed: int = 0) -> dict:
    arg_keys = jax.random.split(jax.random.key(seed), 7)
    act_handoff = scatter_about(arg_keys[0], (N_PIPE, TOK, D), 1.0, 6.0, ((0, 4), (1, 4), (2, 2)))
    grad_handoff = scatter_about(arg_keys[1], (N_PIPE, TOK, D), 1.0, 6.0, ((0, 4), (1, 4), (2, 2)))
    up_blocks = scatter_about(arg_keys[2], (N_PIPE, N_ROW, N_COL, CAP, BLK * BLK), (D // 2) ** -0.5, 0.125, ((0, 4), (1, 2), (2, 4)))
    down_blocks = scatter_about(arg_keys[3], (N_PIPE, N_ROW, N_COL, CAP, BLK * BLK), (FF // 2) ** -0.5, 0.0625, ((0, 4), (1, 2), (2, 4)))
    up_mask = draw_up_mask(jax.random.fold_in(arg_keys[6], 71), 0)
    down_mask = draw_down_mask(jax.random.fold_in(arg_keys[6], 71), 0)
    return dict(act_handoff=act_handoff, grad_handoff=grad_handoff, up_blocks=up_blocks, down_blocks=down_blocks, up_mask=up_mask, down_mask=down_mask)


def slope_of(value):
    sigma = jax.nn.sigmoid(value)
    return sigma * (1.0 + value * (1.0 - sigma))


def unpack_one(packed, live):
    slots = (jnp.cumsum(live) - live).astype(jnp.int32)
    slots = jnp.minimum(slots, CAP - 1)
    return jnp.take(packed, slots, axis=0) * live[:, None].astype(jnp.bfloat16)


def pack_one(blocks, live):
    slots = (jnp.cumsum(live) - live).astype(jnp.int32)
    onehot = (slots[:, None] == jnp.arange(CAP, dtype=jnp.int32)[None, :]) & (live[:, None] > 0)
    source = jnp.sum(jnp.where(onehot, jnp.arange(TILE, dtype=jnp.int32)[:, None], 0), axis=0).astype(jnp.int32)
    filled = jnp.any(onehot, axis=0)
    picked = jnp.take(blocks, source, axis=0)
    return jnp.where(filled[:, None], picked, 0.0).astype(jnp.bfloat16)


def rounded_sum(partials):
    return lax.optimization_barrier(partials.astype(jnp.bfloat16)).astype(jnp.float32).sum(0)


def one_section(operands):
    tokens, grads, up_packed, down_packed, up_live, down_live = operands
    live_up = up_live.reshape(N_ROW, TBR, N_COL, TBC).transpose(0, 2, 1, 3).reshape(N_ROW, N_COL, TILE)
    live_down = down_live.reshape(N_COL, TBC, N_ROW, TBR).transpose(2, 0, 1, 3).reshape(N_ROW, N_COL, TILE)
    up_tiles = jax.vmap(jax.vmap(unpack_one))(up_packed, live_up)
    down_tiles = jax.vmap(jax.vmap(unpack_one))(down_packed, live_down)
    up_dense = up_tiles.reshape(N_ROW, N_COL, TBR, TBC, BLK, BLK).transpose(0, 2, 4, 1, 3, 5).reshape(D, FF)
    down_dense = down_tiles.reshape(N_ROW, N_COL, TBC, TBR, BLK, BLK).transpose(1, 2, 4, 0, 3, 5).reshape(FF, D)
    width_part = D // N_ROW
    hidden_part = FF // N_COL
    tok_wide = tokens.astype(jnp.float32)
    grad_wide = grads.astype(jnp.float32)
    up_wide = up_dense.astype(jnp.float32)
    down_wide = down_dense.astype(jnp.float32)
    pre = rounded_sum(jnp.einsum("trk,rkf->rtf", tok_wide.reshape(TOK, N_ROW, width_part), up_wide.reshape(N_ROW, width_part, FF)))
    hidden = jax.nn.silu(pre).astype(jnp.bfloat16)
    branch = rounded_sum(jnp.einsum("tcj,cjd->ctd", hidden.astype(jnp.float32).reshape(TOK, N_COL, hidden_part), down_wide.reshape(N_COL, hidden_part, D)))
    output = (tok_wide + branch).astype(jnp.bfloat16)
    hidden_grad = rounded_sum(jnp.einsum("trk,frk->rtf", grad_wide.reshape(TOK, N_ROW, width_part), down_wide.reshape(FF, N_ROW, width_part)))
    pre_grad = (hidden_grad * slope_of(pre)).astype(jnp.bfloat16)
    back_branch = rounded_sum(jnp.einsum("tcj,dcj->ctd", pre_grad.astype(jnp.float32).reshape(TOK, N_COL, hidden_part), up_wide.reshape(D, N_COL, hidden_part)))
    in_grad = (grad_wide + back_branch).astype(jnp.bfloat16)
    up_full = jnp.dot(tokens.T, pre_grad, preferred_element_type=jnp.float32)
    down_full = jnp.dot(hidden.T, grads, preferred_element_type=jnp.float32)
    up_cut = up_full.reshape(N_ROW, TBR, BLK, N_COL, TBC, BLK).transpose(0, 3, 1, 4, 2, 5).reshape(N_ROW, N_COL, TILE, BLK * BLK)
    down_cut = down_full.reshape(N_COL, TBC, BLK, N_ROW, TBR, BLK).transpose(3, 0, 1, 4, 2, 5).reshape(N_ROW, N_COL, TILE, BLK * BLK)
    up_packed_grad = jax.vmap(jax.vmap(pack_one))(up_cut, live_up)
    down_packed_grad = jax.vmap(jax.vmap(pack_one))(down_cut, live_down)
    return output, in_grad, up_packed_grad, down_packed_grad


def reference(act_handoff, grad_handoff, up_blocks, down_blocks, up_mask, down_mask):
    section_in = jnp.roll(act_handoff, 1, axis=0)
    grad_back = jnp.roll(grad_handoff, -1, axis=0)
    outputs = lax.map(one_section, (section_in, grad_back, up_blocks, down_blocks, up_mask, down_mask))
    return (outputs[0], outputs[1], outputs[2], outputs[3])
```

```python
import functools
import jax
import jax.numpy as jnp
from jax import lax
from jax.experimental import pallas as pl
from jax.experimental.pallas import tpu as pltpu
from jax.sharding import PartitionSpec as P

BLK = 64
LANES = 128
PADROWS = 9


def low_half(rows):
    return lax.broadcasted_iota(jnp.int32, (rows, LANES), 1) < BLK


def largest_part(total, most):
    return max(part for part in range(1, most + 1) if total % part == 0)


def unpack_kernel(slot_ref, packed_ref, out_ref, raw_ref, stage_ref, sems, *, cols, capacity, group):
    pitch = capacity + PADROWS
    half = BLK // 2
    part = pl.program_id(0)
    step = pl.program_id(1)
    pieces = sems.shape[1]
    piece = capacity // pieces
    chunk = 64

    def fetch(h, p):
        return pltpu.make_async_copy(
            packed_ref.at[pl.ds(p * piece, piece), pl.ds(h * half * BLK, half * BLK)],
            raw_ref.at[h, pl.ds(p * piece, piece), :], sems.at[h, p])

    @pl.when((part == 0) & (step == 0))
    def _():
        for h in range(2):
            for p in range(pieces):
                fetch(h, p).start()
        for i in range(half):
            stage_ref[pl.ds(i * pitch + capacity, 8), :] = jnp.zeros((8, LANES), jnp.float32)

    def stage_half(h):
        keep = low_half(chunk)

        def stage(at, carry):
            base = pl.multiple_of(at * chunk, chunk)
            for tile in range(half // 2):
                value = raw_ref[h, pl.ds(base, chunk), tile * LANES:(tile + 1) * LANES].astype(jnp.float32)
                swapped = pltpu.roll(value, BLK, 1)
                stage_ref[pl.ds(2 * tile * pitch + base, chunk), :] = jnp.where(keep, value, swapped)
                stage_ref[pl.ds((2 * tile + 1) * pitch + base, chunk), :] = jnp.where(keep, swapped, value)
            return carry

        for p in range(pieces):
            fetch(h, p).wait()
            lax.fori_loop(p * piece // chunk, (p + 1) * piece // chunk, stage, 0)

    for h in range(2):
        pl.when((part == h) & (step == 0))(functools.partial(stage_half, h))

    keep = low_half(half)

    def block_row(r, carry):
        at = (step * group + r) * cols
        for pair in range(cols // 2):
            left = stage_ref[pl.ds(slot_ref[at + 2 * pair], half, stride=pitch), :]
            right = stage_ref[pl.ds(slot_ref[at + 2 * pair + 1], half, stride=pitch), :]
            out_ref[r, 0, :, pair * LANES:(pair + 1) * LANES] = jnp.where(keep, left, right).astype(jnp.bfloat16)
        return carry

    lax.fori_loop(0, group, block_row, 0)


def unpack(packed, slots, rows, cols):
    capacity = packed.shape[0]
    pitch = capacity + PADROWS
    half = BLK // 2
    group = largest_part(rows, 8)
    dense = pl.pallas_call(
        functools.partial(unpack_kernel, cols=cols, capacity=capacity, group=group),
        out_shape=jax.ShapeDtypeStruct((rows, 2, half, cols * BLK), jnp.bfloat16),
        grid_spec=pltpu.PrefetchScalarGridSpec(
            num_scalar_prefetch=1,
            grid=(2, rows // group),
            in_specs=[pl.BlockSpec(memory_space=pl.ANY)],
            out_specs=pl.BlockSpec((group, 1, half, cols * BLK), lambda h, r, s: (r, h, 0, 0)),
            scratch_shapes=[
                pltpu.VMEM((2, capacity, half * BLK), jnp.bfloat16),
                pltpu.VMEM((half * pitch, LANES), jnp.float32),
                pltpu.SemaphoreType.DMA((2, 4)),
            ],
        ),
        compiler_params=pltpu.CompilerParams(
            dimension_semantics=("arbitrary", "arbitrary"), vmem_limit_bytes=60 << 20
        ),
        name="unpack_tile",
    )(slots, packed)
    return dense.reshape(rows * BLK, cols * BLK)


def grad_kernel(slot_ref, count_ref, lhs_ref, rhs_ref, out_ref, turned_ref, even_ref, odd_ref, stage_ref, *,
                group, groups, cols, capacity, width, pairs, chunks):
    pitch = capacity + PADROWS
    half = BLK // 2
    step = pl.program_id(0)
    keep = low_half(half)

    def multiply(n, res_ref):
        base = pl.multiple_of(n * (pairs * LANES), pairs * LANES)
        value = jnp.dot(turned_ref[...], rhs_ref[:, pl.ds(base, pairs * LANES)], preferred_element_type=jnp.float32)
        for q in range(pairs):
            res_ref[q] = value[:, q * LANES:(q + 1) * LANES]

    def scatter(at, res_ref):
        valid = at >= 0
        at = jnp.maximum(at, 0)
        block_row = at // chunks * group
        block_col = at % chunks * (2 * pairs)
        for r in range(group):
            for q in range(pairs):
                even = res_ref[q, pl.ds(r * BLK, half, stride=2), :]
                odd = res_ref[q, pl.ds(r * BLK + 1, half, stride=2), :]
                first = jnp.where(keep, even, pltpu.roll(odd, BLK, 1))
                second = jnp.where(keep, pltpu.roll(even, BLK, 1), odd)
                where = (block_row + r) * cols + block_col + 2 * q
                one = jnp.where(valid, slot_ref[where], capacity)
                two = jnp.where(valid, slot_ref[where + 1], capacity)
                stage_ref[pl.ds(one, half, stride=pitch), :] = first
                stage_ref[pl.ds(two, half, stride=pitch), :] = second

    @pl.when(step < groups)
    def _():
        turned_ref[...] = lhs_ref[...].T
        if chunks % 2:
            def one_chunk(n, carry):
                multiply(n, even_ref)
                scatter(step * chunks + n, even_ref)
                return carry

            lax.fori_loop(0, chunks, one_chunk, 0)
        else:
            def two_chunks(m, carry):
                at = step * chunks + 2 * m
                multiply(2 * m, even_ref)
                scatter(at - 1, odd_ref)
                multiply(2 * m + 1, odd_ref)
                scatter(at, even_ref)
                return carry

            lax.fori_loop(0, chunks // 2, two_chunks, 0)

    if chunks % 2 == 0:
        @pl.when(step == groups)
        def _():
            scatter(groups * chunks - 1, odd_ref)

    @pl.when(step >= groups)
    def _():
        count = count_ref[0]
        chunk = 64
        tiles = width // LANES
        first_tile = (step - groups) * tiles

        def emit(s, carry):
            base = pl.multiple_of(s * chunk, chunk)
            live = lax.broadcasted_iota(jnp.int32, (chunk, LANES), 0) + base < count
            for t in range(tiles):
                value = stage_ref[pl.ds((first_tile + t) * pitch + base, chunk), :]
                out_ref[pl.ds(base, chunk), t * LANES:(t + 1) * LANES] = jnp.where(live, value, 0.0).astype(jnp.bfloat16)
            return carry

        lax.fori_loop(0, capacity // chunk, emit, 0)


def packed_grad(lhs, rhs, slots, count, rows, cols, capacity):
    tokens = lhs.shape[0]
    pitch = capacity + PADROWS
    half = BLK // 2
    group = max(g for g in range(1, 9) if rows % g == 0 and g * BLK % LANES == 0 or g == rows)
    groups = rows // group
    pairs = 2 if cols % 4 == 0 else 1
    width = 1024
    span = group * BLK
    emits = BLK * BLK // width
    return pl.pallas_call(
        functools.partial(grad_kernel, group=group, groups=groups, cols=cols, capacity=capacity, width=width,
                          pairs=pairs, chunks=cols // (2 * pairs)),
        out_shape=jax.ShapeDtypeStruct((capacity, BLK * BLK), jnp.bfloat16),
        grid_spec=pltpu.PrefetchScalarGridSpec(
            num_scalar_prefetch=2,
            grid=(groups + emits,),
            in_specs=[
                pl.BlockSpec((tokens, span), lambda s, a, b: (0, jnp.minimum(s, groups - 1))),
                pl.BlockSpec((tokens, cols * BLK), lambda s, a, b: (0, 0)),
            ],
            out_specs=pl.BlockSpec((capacity, width), lambda s, a, b: (0, jnp.maximum(s - groups, 0))),
            scratch_shapes=[
                pltpu.VMEM((span, tokens), jnp.bfloat16),
                pltpu.VMEM((pairs, span, LANES), jnp.float32),
                pltpu.VMEM((pairs, span, LANES), jnp.float32),
                pltpu.VMEM((half * pitch, LANES), jnp.float32),
            ],
        ),
        compiler_params=pltpu.CompilerParams(
            dimension_semantics=("arbitrary",), vmem_limit_bytes=50 << 20
        ),
        name="packed_grad",
    )(slots, count, lhs, rhs)


def moved(value, axis, pairs):
    return lax.ppermute(value, axis, pairs)


def shifted(value, axis, steps):
    count = lax.axis_size(axis)
    return moved(value, axis, [(source, (source + steps) % count) for source in range(count)])


def row_others(part):
    return [shifted(part, "row", steps) for steps in range(1, lax.axis_size("row"))]


def wide_sum(parts):
    total = parts[0].astype(jnp.float32)
    for part in parts[1:]:
        total = total + part.astype(jnp.float32)
    return total


def slope_of(value):
    sigma = jax.nn.sigmoid(value)
    return sigma * (1.0 + value * (1.0 - sigma))


def slots_of(grid, capacity):
    live = grid.reshape(-1)
    slots = jnp.cumsum(live) - live
    return jnp.where(live > 0, slots, capacity).astype(jnp.int32), jnp.sum(live, keepdims=True)


def product(left, right, dims):
    return lax.dot_general(left, right, (dims, ((), ())), preferred_element_type=jnp.float32).astype(jnp.bfloat16)


UPWARD = [(0, 1), (1, 2), (2, 3)]
DOWNWARD = [(1, 0), (2, 1), (3, 2)]
OUTWARD = [(1, 0), (2, 3)]


def after(value, *earlier):
    return lax.optimization_barrier((value, *earlier))[0]


def direct_scatter(part):
    count = lax.axis_size("col")
    rows = part.shape[0] // count
    own = part[:rows]
    return [own] + [shifted(part[d * rows:(d + 1) * rows], "col", d) for d in range(1, count)]


def direct_gather(value):
    others = [shifted(value, "col", -d) for d in range(1, lax.axis_size("col"))]
    return jnp.concatenate([value] + others, axis=0)


def near_gather(value, waits):
    if lax.axis_size("col") != 4:
        return direct_gather(value)
    place = lax.axis_index("col")
    opposite = shifted(value, "col", 2)
    above = moved(value, "col", DOWNWARD)
    below = moved(value, "col", UPWARD)
    far = moved(after(opposite, *waits), "col", OUTWARD)
    return jnp.concatenate(
        [value, jnp.where(place == 3, far, above), opposite, jnp.where(place == 0, far, below)], axis=0)


def body(act_handoff, grad_handoff, up_blocks, down_blocks, up_mask, down_mask):
    capacity = up_blocks.shape[3]
    rows, cols = up_mask.shape[1:]
    up_slots, up_count = slots_of(up_mask[0], capacity)
    down_slots, down_count = slots_of(down_mask[0], capacity)
    tok_in = shifted(act_handoff, "pipe", 1)
    grad_in = shifted(after(grad_handoff, tok_in), "pipe", -1)[0]
    tok_in = tok_in[0]
    up = unpack(up_blocks[0, 0, 0], after(up_slots, tok_in), rows, cols)
    tokens = near_gather(tok_in, (up,))
    down = unpack(down_blocks[0, 0, 0], after(down_slots, up), cols, rows)
    part = product(tokens, up, ((1,), (0,)))
    grads = near_gather(after(grad_in, tokens), (part,))
    pre = wide_sum([part] + row_others(part))
    hidden = jax.nn.silu(pre).astype(jnp.bfloat16)
    branch_part = product(hidden, down, ((1,), (0,)))
    branch = direct_scatter(branch_part)
    part = product(after(grads, branch_part), down, ((1,), (1,)))
    hidden_grad = wide_sum([part] + row_others(part))
    pre_grad = (hidden_grad * slope_of(pre)).astype(jnp.bfloat16)
    back_part = product(pre_grad, up, ((1,), (1,)))
    back = direct_scatter(back_part)
    down_grad = packed_grad(after(hidden, back_part), grads, down_slots, down_count, cols, rows, capacity)
    up_grad = packed_grad(after(tokens, down_grad), pre_grad, up_slots, up_count, rows, cols, capacity)
    section_output = wide_sum([tok_in] + branch).astype(jnp.bfloat16)[None]
    input_grad = wide_sum([grad_in] + back).astype(jnp.bfloat16)[None]
    return (section_output, input_grad, up_grad[None, None, None], down_grad[None, None, None])


def solution(mesh):
    return jax.shard_map(
        body,
        mesh=mesh,
        in_specs=(
            P("pipe", "col", "row"),
            P("pipe", "col", "row"),
            P("pipe", "row", "col", None, None),
            P("pipe", "row", "col", None, None),
            P("pipe", "row", "col"),
            P("pipe", "col", "row"),
        ),
        out_specs=(
            P("pipe", "col", "row"),
            P("pipe", "col", "row"),
            P("pipe", "row", "col", None, None),
            P("pipe", "row", "col", None, None),
        ),
        check_vma=False,
    )
```

```python
import functools
import jax
import jax.numpy as jnp
from jax import lax
from jax.experimental import pallas as pl
from jax.experimental.pallas import tpu as pltpu
from jax.sharding import PartitionSpec as P

BLK = 64
LANES = 128
PADROWS = 9


def low_half(rows):
    return lax.broadcasted_iota(jnp.int32, (rows, LANES), 1) < BLK


def largest_part(total, most):
    return max(part for part in range(1, most + 1) if total % part == 0)


def unpack_kernel(slot_ref, packed_ref, out_ref, raw_ref, stage_ref, sems, *, cols, capacity, group):
    pitch = capacity + PADROWS
    half = BLK // 2
    part = pl.program_id(0)
    step = pl.program_id(1)
    pieces = sems.shape[1]
    piece = capacity // pieces
    chunk = 64

    def fetch(h, p):
        return pltpu.make_async_copy(
            packed_ref.at[pl.ds(p * piece, piece), pl.ds(h * half * BLK, half * BLK)],
            raw_ref.at[h, pl.ds(p * piece, piece), :], sems.at[h, p])

    @pl.when((part == 0) & (step == 0))
    def _():
        for h in range(2):
            for p in range(pieces):
                fetch(h, p).start()
        for i in range(half):
            stage_ref[pl.ds(i * pitch + capacity, 8), :] = jnp.zeros((8, LANES), jnp.float32)

    def stage_half(h):
        keep = low_half(chunk)

        def stage(at, carry):
            base = pl.multiple_of(at * chunk, chunk)
            for tile in range(half // 2):
                value = raw_ref[h, pl.ds(base, chunk), tile * LANES:(tile + 1) * LANES].astype(jnp.float32)
                swapped = pltpu.roll(value, BLK, 1)
                stage_ref[pl.ds(2 * tile * pitch + base, chunk), :] = jnp.where(keep, value, swapped)
                stage_ref[pl.ds((2 * tile + 1) * pitch + base, chunk), :] = jnp.where(keep, swapped, value)
            return carry

        for p in range(pieces):
            fetch(h, p).wait()
            lax.fori_loop(p * piece // chunk, (p + 1) * piece // chunk, stage, 0)

    for h in range(2):
        pl.when((part == h) & (step == 0))(functools.partial(stage_half, h))

    keep = low_half(half)

    def block_row(r, carry):
        at = (step * group + r) * cols
        for pair in range(cols // 2):
            left = stage_ref[pl.ds(slot_ref[at + 2 * pair], half, stride=pitch), :]
            right = stage_ref[pl.ds(slot_ref[at + 2 * pair + 1], half, stride=pitch), :]
            out_ref[r, 0, :, pair * LANES:(pair + 1) * LANES] = jnp.where(keep, left, right).astype(jnp.bfloat16)
        return carry

    lax.fori_loop(0, group, block_row, 0)


def unpack(packed, slots, rows, cols):
    capacity = packed.shape[0]
    pitch = capacity + PADROWS
    half = BLK // 2
    group = largest_part(rows, 8)
    dense = pl.pallas_call(
        functools.partial(unpack_kernel, cols=cols, capacity=capacity, group=group),
        out_shape=jax.ShapeDtypeStruct((rows, 2, half, cols * BLK), jnp.bfloat16),
        grid_spec=pltpu.PrefetchScalarGridSpec(
            num_scalar_prefetch=1,
            grid=(2, rows // group),
            in_specs=[pl.BlockSpec(memory_space=pl.ANY)],
            out_specs=pl.BlockSpec((group, 1, half, cols * BLK), lambda h, r, s: (r, h, 0, 0)),
            scratch_shapes=[
                pltpu.VMEM((2, capacity, half * BLK), jnp.bfloat16),
                pltpu.VMEM(((half + 1) * pitch, LANES), jnp.float32),
                pltpu.SemaphoreType.DMA((2, 4)),
            ],
        ),
        compiler_params=pltpu.CompilerParams(
            dimension_semantics=("arbitrary", "arbitrary"), vmem_limit_bytes=60 << 20
        ),
        name="unpack_tile",
    )(slots, packed)
    return dense.reshape(rows * BLK, cols * BLK)


def parted(rows):
    to = lax.broadcasted_iota(jnp.int32, (rows, rows), 0)
    half = BLK // 2
    source = to // BLK * BLK + to % half * 2 + to % BLK // half
    return (lax.broadcasted_iota(jnp.int32, (rows, rows), 1) == source).astype(jnp.bfloat16)


def grad_kernel(slot_ref, count_ref, lhs_ref, rhs_ref, out_ref, turned_ref, even_ref, odd_ref, stage_ref, *,
                group, groups, cols, capacity, width, pairs, chunks):
    pitch = capacity + PADROWS
    half = BLK // 2
    step = pl.program_id(0)
    span = group * BLK
    keep = low_half(half)
    buffers = (even_ref, odd_ref)

    def multiply(n):
        res_ref = buffers[n % 2]
        value = jnp.dot(turned_ref[...], rhs_ref[:, n * pairs * LANES:(n + 1) * pairs * LANES],
                        preferred_element_type=jnp.float32)
        for q in range(pairs):
            res_ref[q] = value[:, q * LANES:(q + 1) * LANES]

    def scatter(n):
        res_ref = buffers[n % 2]
        for r in range(group):
            for q in range(pairs):
                even = res_ref[q, r * BLK:r * BLK + half, :]
                odd = res_ref[q, r * BLK + half:(r + 1) * BLK, :]
                first = jnp.where(keep, even, pltpu.roll(odd, BLK, 1))
                second = jnp.where(keep, pltpu.roll(even, BLK, 1), odd)
                at = (step * group + r) * cols + 2 * (n * pairs + q)
                stage_ref[pl.ds(slot_ref[at], half, stride=pitch), :] = first
                stage_ref[pl.ds(slot_ref[at + 1], half, stride=pitch), :] = second

    @pl.when(step < groups)
    def _():
        part = 2 * BLK if span % (2 * BLK) == 0 else BLK
        order = parted(part)
        for m in range(span // part):
            turned_ref[m * part:(m + 1) * part, :] = lax.dot_general(
                order, lhs_ref[:, m * part:(m + 1) * part], (((1,), (1,)), ((), ())),
                preferred_element_type=jnp.float32).astype(jnp.bfloat16)
        for n in range(chunks):
            multiply(n)
            if n:
                scatter(n - 1)
        scatter(chunks - 1)

    @pl.when(step >= groups)
    def _():
        count = count_ref[0]
        chunk = 64
        tiles = width // LANES
        first_tile = (step - groups) * tiles

        def emit(s, carry):
            base = pl.multiple_of(s * chunk, chunk)
            live = lax.broadcasted_iota(jnp.int32, (chunk, LANES), 0) + base < count
            for t in range(tiles):
                value = stage_ref[pl.ds((first_tile + t) * pitch + base, chunk), :]
                out_ref[pl.ds(base, chunk), t * LANES:(t + 1) * LANES] = jnp.where(live, value, 0.0).astype(jnp.bfloat16)
            return carry

        lax.fori_loop(0, capacity // chunk, emit, 0)


def packed_grad(lhs, rhs, slots, count, rows, cols, capacity):
    tokens = lhs.shape[0]
    pitch = capacity + PADROWS
    half = BLK // 2
    group = max(g for g in range(1, 9) if rows % g == 0 and g * BLK % LANES == 0 or g == rows)
    groups = rows // group
    pairs = max(p for p in (1, 2, 4) if cols % (2 * p) == 0)
    width = 1024
    span = group * BLK
    emits = BLK * BLK // width
    return pl.pallas_call(
        functools.partial(grad_kernel, group=group, groups=groups, cols=cols, capacity=capacity, width=width,
                          pairs=pairs, chunks=cols // (2 * pairs)),
        out_shape=jax.ShapeDtypeStruct((capacity, BLK * BLK), jnp.bfloat16),
        grid_spec=pltpu.PrefetchScalarGridSpec(
            num_scalar_prefetch=2,
            grid=(groups + emits,),
            in_specs=[
                pl.BlockSpec((tokens, span), lambda s, a, b: (0, jnp.minimum(s, groups - 1))),
                pl.BlockSpec((tokens, cols * BLK), lambda s, a, b: (0, 0)),
            ],
            out_specs=pl.BlockSpec((capacity, width), lambda s, a, b: (0, jnp.maximum(s - groups, 0))),
            scratch_shapes=[
                pltpu.VMEM((span, tokens), jnp.bfloat16),
                pltpu.VMEM((pairs, span, LANES), jnp.float32),
                pltpu.VMEM((pairs, span, LANES), jnp.float32),
                pltpu.VMEM(((half + 1) * pitch, LANES), jnp.float32),
            ],
        ),
        compiler_params=pltpu.CompilerParams(
            dimension_semantics=("arbitrary",), vmem_limit_bytes=50 << 20
        ),
        name="packed_grad",
    )(slots, count, lhs, rhs)


def moved(value, axis, pairs):
    return lax.ppermute(value, axis, pairs)


def shifted(value, axis, steps):
    count = lax.axis_size(axis)
    return moved(value, axis, [(source, (source + steps) % count) for source in range(count)])


def row_others(part):
    return [shifted(part, "row", steps) for steps in range(1, lax.axis_size("row"))]


def wide_sum(parts):
    total = parts[0].astype(jnp.float32)
    for part in parts[1:]:
        total = total + part.astype(jnp.float32)
    return total


def slope_of(value):
    sigma = jax.nn.sigmoid(value)
    return sigma * (1.0 + value * (1.0 - sigma))


def slots_of(grid, capacity):
    live = grid.reshape(-1)
    slots = jnp.cumsum(live) - live
    return jnp.where(live > 0, slots, capacity).astype(jnp.int32), jnp.sum(live, keepdims=True)


def product(left, right, dims):
    return lax.dot_general(left, right, (dims, ((), ())), preferred_element_type=jnp.float32).astype(jnp.bfloat16)


UPWARD = [(0, 1), (1, 2), (2, 3)]
DOWNWARD = [(1, 0), (2, 1), (3, 2)]
OUTWARD = [(1, 0), (2, 3)]


def after(value, *earlier):
    return lax.optimization_barrier((value, *earlier))[0]


def direct_scatter(part):
    count = lax.axis_size("col")
    rows = part.shape[0] // count
    own = part[:rows]
    return [own] + [shifted(part[d * rows:(d + 1) * rows], "col", d) for d in range(1, count)]


def direct_gather(value):
    others = [shifted(value, "col", -d) for d in range(1, lax.axis_size("col"))]
    return jnp.concatenate([value] + others, axis=0)


def near_gather(value, waits):
    if lax.axis_size("col") != 4:
        return direct_gather(value)
    place = lax.axis_index("col")
    opposite = shifted(value, "col", 2)
    above = moved(value, "col", DOWNWARD)
    below = moved(value, "col", UPWARD)
    far = moved(after(opposite, *waits), "col", OUTWARD)
    return jnp.concatenate(
        [value, jnp.where(place == 3, far, above), opposite, jnp.where(place == 0, far, below)], axis=0)


def body(act_handoff, grad_handoff, up_blocks, down_blocks, up_mask, down_mask):
    capacity = up_blocks.shape[3]
    rows, cols = up_mask.shape[1:]
    up_slots, up_count = slots_of(up_mask[0], capacity)
    down_slots, down_count = slots_of(down_mask[0], capacity)
    tok_in = shifted(act_handoff, "pipe", 1)
    up = unpack(up_blocks[0, 0, 0], up_slots, rows, cols)
    tok_in = after(tok_in, up)
    grad_in = shifted(after(grad_handoff, tok_in), "pipe", -1)[0]
    tok_in = tok_in[0]
    down = unpack(down_blocks[0, 0, 0], after(down_slots, tok_in), cols, rows)
    tokens = near_gather(tok_in, (down,))
    part = product(tokens, up, ((1,), (0,)))
    grads = near_gather(after(grad_in, down), (part,))
    pre = wide_sum([part] + row_others(part))
    hidden = jax.nn.silu(pre).astype(jnp.bfloat16)
    branch_part = product(hidden, down, ((1,), (0,)))
    branch = direct_scatter(branch_part)
    part = product(after(grads, branch_part), down, ((1,), (1,)))
    hidden_grad = wide_sum([part] + row_others(part))
    pre_grad = (hidden_grad * slope_of(pre)).astype(jnp.bfloat16)
    back_part = product(pre_grad, up, ((1,), (1,)))
    back = direct_scatter(back_part)
    down_grad = packed_grad(after(hidden, back_part), grads, down_slots, down_count, cols, rows, capacity)
    up_grad = packed_grad(after(tokens, down_grad), pre_grad, up_slots, up_count, rows, cols, capacity)
    section_output = wide_sum([tok_in] + branch).astype(jnp.bfloat16)[None]
    input_grad = wide_sum([grad_in] + back).astype(jnp.bfloat16)[None]
    return (section_output, input_grad, up_grad[None, None, None], down_grad[None, None, None])


def solution(mesh):
    return jax.shard_map(
        body,
        mesh=mesh,
        in_specs=(
            P("pipe", "col", "row"),
            P("pipe", "col", "row"),
            P("pipe", "row", "col", None, None),
            P("pipe", "row", "col", None, None),
            P("pipe", "row", "col"),
            P("pipe", "col", "row"),
        ),
        out_specs=(
            P("pipe", "col", "row"),
            P("pipe", "col", "row"),
            P("pipe", "row", "col", None, None),
            P("pipe", "row", "col", None, None),
        ),
        check_vma=False,
    )
```

```python
import functools
import jax
import jax.numpy as jnp
from jax import lax
from jax.experimental import pallas as pl
from jax.experimental.pallas import tpu as pltpu
from jax.sharding import PartitionSpec as P

BLK = 64
LANES = 128
PADROWS = 9


def low_half(rows):
    return lax.broadcasted_iota(jnp.int32, (rows, LANES), 1) < BLK


def largest_part(total, most):
    return max(part for part in range(1, most + 1) if total % part == 0)


def unpack_kernel(slot_ref, packed_ref, out_ref, raw_ref, stage_ref, sems, *, cols, capacity, group):
    pitch = capacity + PADROWS
    half = BLK // 2
    part = pl.program_id(0)
    step = pl.program_id(1)
    pieces = sems.shape[1]
    piece = capacity // pieces
    chunk = 64

    def fetch(h, p):
        return pltpu.make_async_copy(
            packed_ref.at[pl.ds(p * piece, piece), pl.ds(h * half * BLK, half * BLK)],
            raw_ref.at[h, pl.ds(p * piece, piece), :], sems.at[h, p])

    @pl.when((part == 0) & (step == 0))
    def _():
        for h in range(2):
            for p in range(pieces):
                fetch(h, p).start()
        for i in range(half):
            stage_ref[pl.ds(i * pitch + capacity, 8), :] = jnp.zeros((8, LANES), jnp.float32)

    def stage_half(h):
        keep = low_half(chunk)

        def stage(at, carry):
            base = pl.multiple_of(at * chunk, chunk)
            for tile in range(half // 2):
                value = raw_ref[h, pl.ds(base, chunk), tile * LANES:(tile + 1) * LANES].astype(jnp.float32)
                swapped = pltpu.roll(value, BLK, 1)
                stage_ref[pl.ds(2 * tile * pitch + base, chunk), :] = jnp.where(keep, value, swapped)
                stage_ref[pl.ds((2 * tile + 1) * pitch + base, chunk), :] = jnp.where(keep, swapped, value)
            return carry

        for p in range(pieces):
            fetch(h, p).wait()
            lax.fori_loop(p * piece // chunk, (p + 1) * piece // chunk, stage, 0)

    for h in range(2):
        pl.when((part == h) & (step == 0))(functools.partial(stage_half, h))

    keep = low_half(half)

    def block_row(r, carry):
        at = (step * group + r) * cols
        for pair in range(cols // 2):
            left = stage_ref[pl.ds(slot_ref[at + 2 * pair], half, stride=pitch), :]
            right = stage_ref[pl.ds(slot_ref[at + 2 * pair + 1], half, stride=pitch), :]
            out_ref[r, 0, :, pair * LANES:(pair + 1) * LANES] = jnp.where(keep, left, right).astype(jnp.bfloat16)
        return carry

    lax.fori_loop(0, group, block_row, 0)


def unpack(packed, slots, rows, cols):
    capacity = packed.shape[0]
    pitch = capacity + PADROWS
    half = BLK // 2
    group = largest_part(rows, 16)
    dense = pl.pallas_call(
        functools.partial(unpack_kernel, cols=cols, capacity=capacity, group=group),
        out_shape=jax.ShapeDtypeStruct((rows, 2, half, cols * BLK), jnp.bfloat16),
        grid_spec=pltpu.PrefetchScalarGridSpec(
            num_scalar_prefetch=1,
            grid=(2, rows // group),
            in_specs=[pl.BlockSpec(memory_space=pl.ANY)],
            out_specs=pl.BlockSpec((group, 1, half, cols * BLK), lambda h, r, s: (r, h, 0, 0)),
            scratch_shapes=[
                pltpu.VMEM((2, capacity, half * BLK), jnp.bfloat16),
                pltpu.VMEM(((half + 1) * pitch, LANES), jnp.float32),
                pltpu.SemaphoreType.DMA((2, 4)),
            ],
        ),
        compiler_params=pltpu.CompilerParams(
            dimension_semantics=("arbitrary", "arbitrary"), vmem_limit_bytes=60 << 20
        ),
        name="unpack_tile",
    )(slots, packed)
    return dense.reshape(rows * BLK, cols * BLK)


def unpack_half_kernel(slot_ref, packed_ref, *refs, cols, capacity, group, part):
    out_ref, raw_ref, stage_ref, sems = refs[-4:]
    pitch = capacity + PADROWS
    half = BLK // 2
    step = pl.program_id(0)
    pieces = sems.shape[0]
    piece = capacity // pieces

    @pl.when(step == 0)
    def _():
        chunk = 32
        copies = [
            pltpu.make_async_copy(
                packed_ref.at[pl.ds(p * piece, piece), pl.ds(part * half * BLK, half * BLK)],
                raw_ref.at[pl.ds(p * piece, piece), :], sems.at[p])
            for p in range(pieces)
        ]
        for copy in copies:
            copy.start()
        for i in range(half):
            stage_ref[pl.ds(i * pitch + capacity, 8), :] = jnp.zeros((8, LANES), jnp.float32)

        keep = low_half(chunk)

        def stage(at, carry):
            base = pl.multiple_of(at * chunk, chunk)
            for tile in range(half // 2):
                value = raw_ref[pl.ds(base, chunk), tile * LANES:(tile + 1) * LANES].astype(jnp.float32)
                swapped = pltpu.roll(value, BLK, 1)
                stage_ref[pl.ds(2 * tile * pitch + base, chunk), :] = jnp.where(keep, value, swapped)
                stage_ref[pl.ds((2 * tile + 1) * pitch + base, chunk), :] = jnp.where(keep, swapped, value)
            return carry

        for p, copy in enumerate(copies):
            copy.wait()
            lax.fori_loop(p * piece // chunk, (p + 1) * piece // chunk, stage, 0)

    keep = low_half(half)

    def block_row(r, carry):
        at = (step * group + r) * cols
        for pair in range(cols // 2):
            left = stage_ref[pl.ds(slot_ref[at + 2 * pair], half, stride=pitch), :]
            right = stage_ref[pl.ds(slot_ref[at + 2 * pair + 1], half, stride=pitch), :]
            out_ref[r, 0, :, pair * LANES:(pair + 1) * LANES] = jnp.where(keep, left, right).astype(jnp.bfloat16)
        return carry

    lax.fori_loop(0, group, block_row, 0)


def unpack_half(packed, slots, rows, cols, part, previous=None):
    capacity = packed.shape[0]
    half = BLK // 2
    group = largest_part(rows, 16)
    anywhere = pl.BlockSpec(memory_space=pl.ANY)
    given = () if previous is None else (previous,)
    return pl.pallas_call(
        functools.partial(unpack_half_kernel, cols=cols, capacity=capacity, group=group, part=part),
        out_shape=jax.ShapeDtypeStruct((rows, 2, half, cols * BLK), jnp.bfloat16),
        grid_spec=pltpu.PrefetchScalarGridSpec(
            num_scalar_prefetch=1,
            grid=(rows // group,),
            in_specs=[anywhere] * (1 + len(given)),
            out_specs=pl.BlockSpec((group, 1, half, cols * BLK), lambda r, s: (r, part, 0, 0)),
            scratch_shapes=[
                pltpu.VMEM((capacity, half * BLK), jnp.bfloat16),
                pltpu.VMEM(((half + 1) * (capacity + PADROWS), LANES), jnp.float32),
                pltpu.SemaphoreType.DMA((4,)),
            ],
        ),
        input_output_aliases={2: 0} if given else {},
        compiler_params=pltpu.CompilerParams(dimension_semantics=("arbitrary",), vmem_limit_bytes=60 << 20),
        name="unpack_half",
    )(slots, packed, *given)


def parted(rows):
    to = lax.broadcasted_iota(jnp.int32, (rows, rows), 0)
    half = BLK // 2
    source = to // BLK * BLK + to % half * 2 + to % BLK // half
    return (lax.broadcasted_iota(jnp.int32, (rows, rows), 1) == source).astype(jnp.bfloat16)


def grad_kernel(slot_ref, count_ref, lhs_ref, rhs_ref, out_ref, turned_ref, even_ref, odd_ref, stage_ref, *,
                group, groups, cols, capacity, width, pairs, chunks):
    pitch = capacity + PADROWS
    half = BLK // 2
    step = pl.program_id(0)
    span = group * BLK
    keep = low_half(half)
    buffers = (even_ref, odd_ref)

    def multiply(n):
        res_ref = buffers[n % 2]
        value = jnp.dot(turned_ref[...], rhs_ref[:, n * pairs * LANES:(n + 1) * pairs * LANES],
                        preferred_element_type=jnp.float32)
        for q in range(pairs):
            res_ref[q] = value[:, q * LANES:(q + 1) * LANES]

    def scatter(n):
        res_ref = buffers[n % 2]
        for r in range(group):
            for q in range(pairs):
                even = res_ref[q, r * BLK:r * BLK + half, :]
                odd = res_ref[q, r * BLK + half:(r + 1) * BLK, :]
                first = jnp.where(keep, even, pltpu.roll(odd, BLK, 1))
                second = jnp.where(keep, pltpu.roll(even, BLK, 1), odd)
                at = (step * group + r) * cols + 2 * (n * pairs + q)
                stage_ref[pl.ds(slot_ref[at], half, stride=pitch), :] = first
                stage_ref[pl.ds(slot_ref[at + 1], half, stride=pitch), :] = second

    @pl.when(step < groups)
    def _():
        part = 2 * BLK if span % (2 * BLK) == 0 else BLK
        order = parted(part)
        for m in range(span // part):
            turned_ref[m * part:(m + 1) * part, :] = lax.dot_general(
                order, lhs_ref[:, m * part:(m + 1) * part], (((1,), (1,)), ((), ())),
                preferred_element_type=jnp.float32).astype(jnp.bfloat16)
        for n in range(chunks):
            multiply(n)
            if n:
                scatter(n - 1)
        scatter(chunks - 1)

    @pl.when(step >= groups)
    def _():
        count = count_ref[0]
        chunk = 64
        tiles = width // LANES
        first_tile = (step - groups) * tiles

        def emit(s, carry):
            base = pl.multiple_of(s * chunk, chunk)
            live = lax.broadcasted_iota(jnp.int32, (chunk, LANES), 0) + base < count
            for t in range(tiles):
                value = stage_ref[pl.ds((first_tile + t) * pitch + base, chunk), :]
                out_ref[pl.ds(base, chunk), t * LANES:(t + 1) * LANES] = jnp.where(live, value, 0.0).astype(jnp.bfloat16)
            return carry

        lax.fori_loop(0, capacity // chunk, emit, 0)


def packed_grad(lhs, rhs, slots, count, rows, cols, capacity):
    tokens = lhs.shape[0]
    pitch = capacity + PADROWS
    half = BLK // 2
    group = max(g for g in range(1, 9) if rows % g == 0 and g * BLK % LANES == 0 or g == rows)
    groups = rows // group
    pairs = max(p for p in (1, 2, 4) if cols % (2 * p) == 0)
    width = 1024
    span = group * BLK
    emits = BLK * BLK // width
    return pl.pallas_call(
        functools.partial(grad_kernel, group=group, groups=groups, cols=cols, capacity=capacity, width=width,
                          pairs=pairs, chunks=cols // (2 * pairs)),
        out_shape=jax.ShapeDtypeStruct((capacity, BLK * BLK), jnp.bfloat16),
        grid_spec=pltpu.PrefetchScalarGridSpec(
            num_scalar_prefetch=2,
            grid=(groups + emits,),
            in_specs=[
                pl.BlockSpec((tokens, span), lambda s, a, b: (0, jnp.minimum(s, groups - 1))),
                pl.BlockSpec((tokens, cols * BLK), lambda s, a, b: (0, 0)),
            ],
            out_specs=pl.BlockSpec((capacity, width), lambda s, a, b: (0, jnp.maximum(s - groups, 0))),
            scratch_shapes=[
                pltpu.VMEM((span, tokens), jnp.bfloat16),
                pltpu.VMEM((pairs, span, LANES), jnp.float32),
                pltpu.VMEM((pairs, span, LANES), jnp.float32),
                pltpu.VMEM(((half + 1) * pitch, LANES), jnp.float32),
            ],
        ),
        compiler_params=pltpu.CompilerParams(
            dimension_semantics=("arbitrary",), vmem_limit_bytes=50 << 20
        ),
        name="packed_grad",
    )(slots, count, lhs, rhs)


def moved(value, axis, pairs):
    return lax.ppermute(value, axis, pairs)


def shifted(value, axis, steps):
    count = lax.axis_size(axis)
    return moved(value, axis, [(source, (source + steps) % count) for source in range(count)])


def row_others(part):
    return [shifted(part, "row", steps) for steps in range(1, lax.axis_size("row"))]


def wide_sum(parts):
    total = parts[0].astype(jnp.float32)
    for part in parts[1:]:
        total = total + part.astype(jnp.float32)
    return total


def slope_of(value):
    sigma = jax.nn.sigmoid(value)
    return sigma * (1.0 + value * (1.0 - sigma))


def slots_of(grid, capacity):
    live = grid.reshape(-1)
    slots = jnp.cumsum(live) - live
    return jnp.where(live > 0, slots, capacity).astype(jnp.int32), jnp.sum(live, keepdims=True)


def product(left, right, dims):
    return lax.dot_general(left, right, (dims, ((), ())), preferred_element_type=jnp.float32).astype(jnp.bfloat16)


UPWARD = [(0, 1), (1, 2), (2, 3)]
DOWNWARD = [(1, 0), (2, 1), (3, 2)]
OUTWARD = [(1, 0), (2, 3)]


def after(value, *earlier):
    return lax.optimization_barrier((value, *earlier))[0]


def direct_scatter(part):
    count = lax.axis_size("col")
    rows = part.shape[0] // count
    own = part[:rows]
    return [own] + [shifted(part[d * rows:(d + 1) * rows], "col", d) for d in range(1, count)]


def direct_gather(value):
    others = [shifted(value, "col", -d) for d in range(1, lax.axis_size("col"))]
    return jnp.concatenate([value] + others, axis=0)


def near_gather(value, waits):
    if lax.axis_size("col") != 4:
        return direct_gather(value)
    place = lax.axis_index("col")
    opposite = shifted(value, "col", 2)
    above = moved(value, "col", DOWNWARD)
    below = moved(value, "col", UPWARD)
    far = moved(after(opposite, *waits), "col", OUTWARD)
    return jnp.concatenate(
        [value, jnp.where(place == 3, far, above), opposite, jnp.where(place == 0, far, below)], axis=0)


def body(act_handoff, grad_handoff, up_blocks, down_blocks, up_mask, down_mask):
    capacity = up_blocks.shape[3]
    rows, cols = up_mask.shape[1:]
    up_slots, up_count = slots_of(up_mask[0], capacity)
    down_slots, down_count = slots_of(down_mask[0], capacity)
    tok_in = shifted(act_handoff, "pipe", 1)
    up = unpack(up_blocks[0, 0, 0], up_slots, rows, cols)
    tok_in = after(tok_in, up)
    grad_in = shifted(after(grad_handoff, tok_in), "pipe", -1)[0]
    tok_in = tok_in[0]
    down = unpack_half(down_blocks[0, 0, 0], after(down_slots, tok_in), cols, rows, 0)
    tokens = near_gather(tok_in, (down,))
    down = unpack_half(down_blocks[0, 0, 0], down_slots, cols, rows, 1, down)
    down = down.reshape(cols * BLK, rows * BLK)
    part = product(tokens, up, ((1,), (0,)))
    grads = near_gather(after(grad_in, down), (part,))
    pre = wide_sum([part] + row_others(part))
    hidden = jax.nn.silu(pre).astype(jnp.bfloat16)
    branch_part = product(hidden, down, ((1,), (0,)))
    branch = direct_scatter(branch_part)
    part = product(after(grads, branch_part), down, ((1,), (1,)))
    hidden_grad = wide_sum([part] + row_others(part))
    pre_grad = (hidden_grad * slope_of(pre)).astype(jnp.bfloat16)
    back_part = product(pre_grad, up, ((1,), (1,)))
    back = direct_scatter(back_part)
    down_grad = packed_grad(after(hidden, back_part), grads, down_slots, down_count, cols, rows, capacity)
    up_grad = packed_grad(after(tokens, down_grad), pre_grad, up_slots, up_count, rows, cols, capacity)
    section_output = wide_sum([tok_in] + branch).astype(jnp.bfloat16)[None]
    input_grad = wide_sum([grad_in] + back).astype(jnp.bfloat16)[None]
    return (section_output, input_grad, up_grad[None, None, None], down_grad[None, None, None])


def solution(mesh):
    return jax.shard_map(
        body,
        mesh=mesh,
        in_specs=(
            P("pipe", "col", "row"),
            P("pipe", "col", "row"),
            P("pipe", "row", "col", None, None),
            P("pipe", "row", "col", None, None),
            P("pipe", "row", "col"),
            P("pipe", "col", "row"),
        ),
        out_specs=(
            P("pipe", "col", "row"),
            P("pipe", "col", "row"),
            P("pipe", "row", "col", None, None),
            P("pipe", "row", "col", None, None),
        ),
        check_vma=False,
    )
```
